512 devices in a mesh: section: 16 (over z), expert: 32 (over x, y, core).
Axes of the slice: x: 4, y: 4, z: 16, core: 2. Of those that a mesh axis runs over, the one named last changes fastest.
Arguments:
- tokens_in: bfloat16 [16, 512, 4096], P('section', 'expert'), may hold values from -6 to 6
- out_grad: bfloat16 [16, 512, 4096], P('section', 'expert'), may hold values from -6 to 6
- expert_ids: int32 [16, 512, 2], P('section', 'expert'), may hold values from 0 to 7, all different within a row; in each aligned block of 16 rows (0 to 15, 16 to 31, ..., all dimensions but the last counted through in order) at most 8 rows name the same one
- gate_weights: bfloat16 [16, 512, 2], P('section', 'expert'), may hold values from 0.099609375 to 1
- w_gate: bfloat16 [16, 6144, 4096], P('section', 'expert'), may hold values from -0.09375 to 0.09375
- w_up: bfloat16 [16, 6144, 4096], P('section', 'expert'), may hold values from -0.09375 to 0.09375
- w_down: bfloat16 [16, 6144, 4096], P('section', 'expert'), may hold values from -0.09375 to 0.09375
Outputs:
- passed_grad: bfloat16 [16, 512, 4096], P('section', 'expert')
- route_grad: float32 [16, 512, 2], P('section', 'expert')
The draws below stay inside these ranges and needn't reach their ends.
Inputs may be any that keep to these rules, and one draw needn't show every extreme that they name: `expert_ids`: the 2 experts of a token differ. Among the 16 tokens of one device no expert is named by more than 8 tokens, and in some device's rows some expert is named by exactly 8.
All inputs are finite; a program needn't handle non-finite values.
Results may differ from the reference program's by a relative error of at most 0.0057.
Values may be sent and summed in bfloat16 or wider, within the bound.
A program may use at most 64 MiB of HBM per device.

```python
import math
import jax
import jax.numpy as jnp
import numpy as np
from jax import lax

D = 4096
HID = 768
EXPERTS = 8
TOPW = 2
TOK_DEV = 16
Q = 8
TOKENS = 512
LAYERS = 16
N_EXPERT = 32


def levels(own_key, extent, pieces, low, top_value):
    loudness, own = 1.0, jax.random.fold_in(own_key, 6)
    for dim, parts in pieces:
        steps = jnp.exp(jax.random.uniform(jax.random.fold_in(own, dim), (parts,), jnp.float32, low / len(pieces), top_value / len(pieces)))
        loudness = loudness * jnp.repeat(steps, extent[dim] // parts).reshape([-1 if axis == dim else 1 for axis in range(len(extent))])
    return loudness


def assign_block(key, own, number, rows, amount, top, most, skew):
    ranking = jax.random.permutation(key, amount)
    heavy_load, usual = shares(amount, rows * top, most, skew, True), shares(amount, rows * top, most, skew, False)
    places = jnp.arange(amount)

    def named(tallies, rotation):
        used = int((tallies > 0).sum())
        fixed = max(1, used // 4)
        passed = fixed + (places - fixed + rotation * (used - fixed)) % max(1, amount - fixed)
        return jnp.zeros((amount,), jnp.int32).at[ranking[jnp.where(places < fixed, places, passed)]].set(jnp.asarray(tallies, jnp.int32))

    tallies = jnp.where(number % 4 == 0, named(heavy_load, number // 4), named(usual, number - number // 4 - 1))
    mixed = jax.random.permutation(jax.random.fold_in(own, 3), amount)
    source_of, sink = mixed[0:amount // 2 * 2:2], mixed[1:amount // 2 * 2:2]
    slack = jnp.minimum(tallies[source_of] - 1, most - tallies[sink]) // 2
    slack = jnp.where((source_of == ranking[0]) | (sink == ranking[0]) | (tallies[sink] == 0), 0, jnp.maximum(slack, 0))
    passed = jax.random.randint(jax.random.fold_in(own, 4), (amount // 2,), 0, 1 << 20) % (slack + 1)
    tallies = tallies.at[source_of].add(-passed).at[sink].add(passed)
    members = jnp.searchsorted(jnp.cumsum(tallies), jnp.arange(rows * top), side="right").astype(jnp.int32)
    grid = members.reshape(top, rows).T
    grid = grid[jax.random.permutation(jax.random.fold_in(own, 1), rows)]
    rotation = jax.random.randint(jax.random.fold_in(own, 2), (rows, 1), 0, top)
    return jnp.take_along_axis(grid, (jnp.arange(top)[None, :] + rotation) % top, axis=1)


def shares(count, total, limit, skew, full):
    portions = [(1 << 20) // math.isqrt(standing ** skew) + 1 for standing in range(1, count + 1)]
    largest = limit if full else min(limit, max(-(-total // count), total * portions[0] // sum(portions)))
    least = 1 if total - largest >= count - 1 else 0
    given, rest = [largest] + [least] * (count - 1), total - largest - least * (count - 1)
    while rest > 0:
        free = [i for i in range(1, count) if given[i] < largest] or [i for i in range(1, count) if given[i] < limit]
        whole, left = sum([portions[i] for i in free]), rest
        for i in free:
            more = min(limit - given[i], max(1, left * portions[i] // whole), rest)
            given[i] = given[i] + more
            rest = rest - more
    return np.array(given)


def centred(key, shape, spread, most, cuts=(), held_as=jnp.bfloat16):
    result = spread * jax.random.normal(key, shape, jnp.float32)
    if cuts:
        result = result * levels(key, shape, cuts, -0.22, 0.18)
    return jnp.clip(result, -most, most).astype(held_as)


def setup_inputs(seed: int = 0) -> dict:
    streams_of = jax.random.split(jax.random.key(seed), 8)
    tokens_in = centred(streams_of[0], (LAYERS, TOKENS, D), 1.0, 6.0, ((0, 16), (1, 32)))
    out_grad = centred(streams_of[1], (LAYERS, TOKENS, D), 1.0, 6.0, ((0, 16), (1, 32)))
    expert_ids_keys = jax.random.split(jax.random.fold_in(streams_of[2], 1), LAYERS * TOKENS // TOK_DEV)
    expert_ids_turns = jax.random.permutation(jax.random.fold_in(streams_of[2], 3), LAYERS * TOKENS // TOK_DEV)
    expert_ids = jax.vmap(lambda own, number: assign_block(jax.random.fold_in(streams_of[2], 2), own, number, TOK_DEV, EXPERTS, TOPW, Q, 2))(expert_ids_keys, expert_ids_turns).reshape((LAYERS, TOKENS, TOPW))
    gate_weights = jnp.clip(0.099609375 + 0.9003906 * jax.random.uniform(streams_of[3], (LAYERS, TOKENS, TOPW), jnp.float32) ** levels(streams_of[3], (LAYERS, TOKENS, TOPW), ((0, 16), (1, 32)), -0.2, 0.2), 0.099609375, 1.0).astype(jnp.bfloat16)
    w_gate = centred(streams_of[4], (LAYERS, EXPERTS * HID, D), D ** -0.5, 0.09375, ((0, 16), (1, 32)))
    w_up = centred(streams_of[5], (LAYERS, EXPERTS * HID, D), D ** -0.5, 0.09375, ((0, 16), (1, 32)))
    w_down = centred(streams_of[6], (LAYERS, EXPERTS * HID, D), D ** -0.5, 0.09375, ((0, 16), (1, 32)))
    return {"tokens_in": tokens_in, "out_grad": out_grad, "expert_ids": expert_ids, "gate_weights": gate_weights, "w_gate": w_gate, "w_up": w_up, "w_down": w_down}


def layer_grads(inputs, upstream, routes, gate_vals, gate_mat, up_mat, down_mat):
    group_size = N_EXPERT // EXPERTS
    width = HID // group_size
    row_count = min(TOKENS, N_EXPERT * (TOK_DEV // 2))
    dims = (((1,), (1,)), ((), ()))

    def one_expert(carry, expert):
        total, grads_route = carry
        route_hit = routes == expert
        routed = jnp.sum(route_hit.astype(jnp.int32), axis=1)
        gate_col = jnp.sum(jnp.where(route_hit, gate_vals.astype(jnp.float32), jnp.float32(0.0)), axis=1)
        order = jnp.argsort(1 - routed, stable=True)[:row_count].astype(jnp.int32)
        rows_x = inputs[order]
        rows_dy = upstream[order]
        rows_g = gate_col[order]
        start = (expert * HID).astype(jnp.int32)
        w_g = lax.dynamic_slice_in_dim(gate_mat, start, HID, 0)
        w_u = lax.dynamic_slice_in_dim(up_mat, start, HID, 0)
        w_d = lax.dynamic_slice_in_dim(down_mat, start, HID, 0)
        gate_pre = lax.dot_general(rows_x, w_g, dims, preferred_element_type=jnp.float32)
        up_pre = lax.dot_general(rows_x, w_u, dims, preferred_element_type=jnp.float32)
        hidden_grad = lax.dot_general(rows_dy, w_d, dims, preferred_element_type=jnp.float32)
        sigmoid_val = jax.nn.sigmoid(gate_pre)
        activated = gate_pre * sigmoid_val
        slope = sigmoid_val * (1.0 + gate_pre * (1.0 - sigmoid_val))
        scaled = hidden_grad * rows_g[:, None]
        grad_gate = (scaled * up_pre * slope).astype(jnp.bfloat16)
        grad_up = (scaled * activated).astype(jnp.bfloat16)
        left_g = grad_gate.astype(jnp.float32).reshape(row_count, group_size, width)
        left_u = grad_up.astype(jnp.float32).reshape(row_count, group_size, width)
        right_g = w_g.astype(jnp.float32).reshape(group_size, width, D)
        right_u = w_u.astype(jnp.float32).reshape(group_size, width, D)
        partial_value = jnp.einsum("rgh,ghd->rgd", left_g, right_g) + jnp.einsum("rgh,ghd->rgd", left_u, right_u)
        partial_value = lax.optimization_barrier(partial_value.astype(jnp.bfloat16)).astype(jnp.float32)
        total = total.at[order].add(jnp.sum(partial_value, axis=1))
        scores = jnp.sum(activated * up_pre * hidden_grad, axis=1)
        score_full = jnp.zeros((TOKENS,), jnp.float32).at[order].add(scores)
        grads_route = grads_route + jnp.where(route_hit, score_full[:, None], jnp.float32(0.0))
        return (total, grads_route), None

    start_carry = (jnp.zeros((TOKENS, D), jnp.float32), jnp.zeros((TOKENS, TOPW), jnp.float32))
    (total, grads_route), _ = lax.scan(one_expert, start_carry, jnp.arange(EXPERTS, dtype=jnp.int32))
    return total.astype(jnp.bfloat16), grads_route


def reference(tokens_in, out_grad, expert_ids, gate_weights, w_gate, w_up, w_down):
    def per_layer(items):
        return layer_grads(*items)

    input_grad, grads_route = lax.map(per_layer, (tokens_in, out_grad, expert_ids, gate_weights, w_gate, w_up, w_down))
    return jnp.roll(input_grad, -1, axis=0), grads_route
```

```python
import jax
import jax.numpy as jnp
from jax import lax
from jax.experimental import pallas as pl
from jax.experimental.pallas import tpu as pltpu
from jax.sharding import PartitionSpec as P

MESH = pl.DeviceIdType.MESH
BF = jnp.bfloat16
F32 = jnp.float32
NT = (((1,), (1,)), ((), ()))
EXPERTS = 8
Q = 8
LANES = 128
COPIES = 40


def iota(shape, dim):
    return lax.broadcasted_iota(jnp.int32, shape, dim)


def dot_nt(left, right):
    return lax.dot_general(left, right, NT, preferred_element_type=F32)


def resplit(total):
    high = total.astype(BF).astype(F32)
    lane = iota(total.shape, 1)
    return jnp.where(lane < 64, high, total - high).astype(BF)


def kernel(
    x_in, dy_in, ids_in, gw_in, wg_in, wu_in, wd_in, out, route,
    blk, sel, xin, relx, reld, w1, w2, acc, acd, res, rr, rela, relb,
    tb, own, from_m, from_p, add_a, add_b, fin, send, recv, local,
):
    D = x_in.shape[2]
    W = wg_in.shape[1]
    half = D // 2
    sec = lax.axis_index("section")
    secs = lax.axis_size("section")
    me = lax.axis_index("expert")
    core = me % 2
    y = (me // 2) % 4
    x = me // 8
    first = core * y + (1 - core) * x
    second = core * x + (1 - core) * y
    step_a = 8 - 6 * core
    step_b = 2 + 6 * core

    def at(pos_a, pos_b):
        return (sec, core + step_a * (pos_a % 4) + step_b * (pos_b % 4))

    a_up, a_dn = at(first + 1, second), at(first + 3, second)
    b_up, b_dn = at(first, second + 1), at(first, second + 3)
    sib = (sec, me + 1 - 2 * core)
    z_dn = ((sec + secs - 1) % secs, me)
    z_up = ((sec + 1) % secs, me)
    own_e = me // 4

    def expert_at(pos_b):
        pos_b = pos_b % 4
        return (1 - core) * (x * 2 + pos_b // 2) + core * (pos_b * 2 + y // 2)

    peers = [expert_at(second + off) for off in (0, 1, 3, 2)]

    def remote(i, src, dst, dev):
        return pltpu.make_async_remote_copy(
            src_ref=src, dst_ref=dst, send_sem=send.at[i], recv_sem=recv.at[i],
            device_id=dev, device_id_type=MESH,
        )

    lo, hi = pl.ds(0, D), pl.ds(D, D + LANES)
    ra, rb = pl.ds(0, half), pl.ds(half, half + LANES)
    r16 = lambda i: pl.ds(16 * i, 16)

    loads = [
        pltpu.make_async_copy(s, d, local.at[i])
        for i, (s, d) in enumerate(
            [
                (x_in.at[0], blk.at[r16(0), lo]),
                (dy_in.at[0], blk.at[r16(0), pl.ds(D, D)]),
                (wg_in.at[0], w1.at[pl.ds(0, W)]),
                (wu_in.at[0], w1.at[pl.ds(2 * W, W)]),
                (wd_in.at[0], w2.at[pl.ds(0, W)]),
            ]
        )
    ]
    for c in loads:
        c.start()

    barrier = pltpu.get_barrier_semaphore()
    for dev in (a_up, a_dn, b_up, b_dn, sib, z_dn, z_up):
        pl.semaphore_signal(barrier, inc=1, device_id=dev, device_id_type=MESH)

    ids = ids_in[0]
    gates = gw_in[0].astype(F32)
    lane16 = iota((16, LANES), 1)
    table = jnp.zeros((16, LANES), F32)
    for k in range(2):
        table = table + jnp.where(lane16 == ids[:, k : k + 1], gates[:, k : k + 1], 0.0)
    blk[r16(0), pl.ds(2 * D, LANES)] = table.astype(BF)

    pl.semaphore_wait(barrier, 7)
    loads[0].wait()
    loads[1].wait()

    up_x = remote(0, blk.at[r16(0), lo], blk.at[r16(1), lo], a_up)
    up_d = remote(1, blk.at[r16(0), hi], blk.at[r16(1), hi], a_up)
    dn_d = remote(2, blk.at[r16(0), hi], blk.at[r16(2), hi], a_dn)
    dn_x = remote(3, blk.at[r16(0), lo], blk.at[r16(2), lo], a_dn)
    fw_x = remote(4, blk.at[r16(1), lo], blk.at[r16(3), lo], a_up)
    fw_d = remote(5, blk.at[r16(2), hi], blk.at[r16(3), hi], a_dn)
    up_x.start()
    dn_d.start()
    up_d.start()
    dn_x.start()
    halves = [
        remote(6, wg_in.at[0], w1.at[pl.ds(W, W)], sib),
        remote(7, wu_in.at[0], w1.at[pl.ds(3 * W, W)], sib),
        remote(8, wd_in.at[0], w2.at[pl.ds(W, W)], sib),
    ]
    for c in halves:
        c.start()
    up_x.wait_recv()
    fw_x.start()
    dn_d.wait_recv()
    fw_d.start()

    def hits(rows):
        return (blk[rows, pl.ds(2 * D, LANES)].astype(F32) > 0.0).astype(BF)

    def ranks(hit):
        n = hit.shape[0]
        r, c = iota((n, n), 0), iota((n, n), 1)
        lower = ((r // 16 == c // 16) & (c < r)).astype(F32).astype(BF)
        return jnp.dot(lower, hit, preferred_element_type=F32).astype(BF)

    def of_peer(index):
        e = jnp.full(index.shape, peers[3], jnp.int32)
        for j in (2, 1, 0):
            e = jnp.where(index == j, peers[j], e)
        return e

    def cut(size, want):
        return max(d for d in range(LANES, want + 1, LANES) if size % d == 0)

    def select(g):
        hit = hits(pl.ds(32 * g, 32))
        rank = ranks(hit)
        row = iota((64, LANES), 0)
        pick = (iota((64, LANES), 1) == of_peer(row // 16)).astype(F32).astype(BF)
        r, c = iota((64, 32), 0), iota((64, 32), 1)
        good = (dot_nt(pick, hit) > 0.5) & (dot_nt(pick, rank) == (r % 8).astype(F32))
        perm = (good & ((r // 8) % 2 == c // 16)).astype(F32).astype(BF)
        width = cut(2 * D + LANES, 1664)

        @pl.loop(0, (2 * D + LANES) // width)
        def _(i):
            cols = pl.ds(pl.multiple_of(i * width, LANES), width)
            got = jnp.dot(
                perm, blk[pl.ds(32 * g, 32), cols], preferred_element_type=F32
            ).astype(BF)
            xin[r16(g), cols] = got[0:16]
            sel[g, :, cols] = got[16:64]

    def direct(g):
        return [
            remote(9 + g, sel.at[g, r16(0)], xin.at[r16(4 + 2 * g)], b_up),
            remote(11 + g, sel.at[g, r16(1)], xin.at[r16(5 + 2 * g)], b_dn),
        ]

    def opposite(g):
        return [
            remote(13 + g, sel.at[g, r16(2), lo], relx.at[g], b_up),
            remote(15 + g, sel.at[g, r16(2), hi], reld.at[g], b_dn),
        ]

    def onward(g):
        return [
            remote(17 + g, relx.at[g], xin.at[r16(2 + g), lo], b_up),
            remote(19 + g, reld.at[g], xin.at[r16(2 + g), hi], b_dn),
        ]

    def go(copies):
        for c in copies:
            c.start()

    def arrived(copies):
        for c in copies:
            c.wait_recv()

    up_d.wait_recv()
    select(0)
    go(opposite(0))
    go(direct(0))
    dn_x.wait_recv()
    fw_x.wait_recv()
    fw_d.wait_recv()
    select(1)
    go(opposite(1))

    hit = hits(pl.ds(0, 64))
    rank = ranks(hit)
    row = iota((LANES, LANES), 0)
    pick = (iota((LANES, LANES), 1) == of_peer(row // 32)).astype(F32).astype(BF)
    r, c = iota((64, LANES), 0), iota((64, LANES), 1)
    good = (dot_nt(hit, pick) > 0.5) & (dot_nt(rank, pick) == (c % 8).astype(F32))
    place = (good & ((c // 8) % 4 == r // 16)).astype(F32).astype(BF)

    for c, f in zip(opposite(0), onward(0)):
        c.wait_recv()
        f.start()

    def experts(row0, count, dst, middle):
        rows = pl.ds(row0, count)
        depth = 512 if D % 512 == 0 else LANES
        acc[0:count] = jnp.zeros((count, 4 * W), F32)
        acd[0:count] = jnp.zeros((count, 2 * W), F32)

        @pl.loop(0, D // depth)
        def _(k):
            cols = pl.ds(pl.multiple_of(k * depth, LANES), depth)
            cols_d = pl.ds(pl.multiple_of(D + k * depth, LANES), depth)
            acc[0:count] += dot_nt(xin[rows, cols], w1[:, cols])
            acd[0:count] += dot_nt(xin[rows, cols_d], w2[:, cols])

        gate_pre = acc[0:count, 0 : 2 * W]
        up_pre = acc[0:count, 2 * W : 4 * W]
        hidden = acd[0:count]
        side = xin[rows, pl.ds(2 * D, LANES)].astype(F32)
        lane = iota((count, LANES), 1)
        gate = jnp.sum(jnp.where(lane == own_e, side, 0.0), axis=1, keepdims=True)
        sig = jax.nn.sigmoid(gate_pre)
        act = gate_pre * sig
        slope = sig * (1.0 + gate_pre * (1.0 - sig))
        score = jnp.sum(act * up_pre * hidden, axis=1, keepdims=True)
        scaled = hidden * gate
        grads = jnp.concatenate(
            [(scaled * up_pre * slope).astype(BF), (scaled * act).astype(BF)], axis=1
        )
        middle()
        base = 0 if dst is rr else row0

        @pl.loop(0, D // depth)
        def _(k):
            cols = pl.ds(pl.multiple_of(k * depth, LANES), depth)
            dst[pl.ds(base, count), cols] = jnp.dot(
                grads, w1[:, cols], preferred_element_type=F32
            ).astype(BF)

        mine = (lane % 64) == own_e
        dst[pl.ds(base, count), pl.ds(D, LANES)] = resplit(jnp.where(mine, score, 0.0))

    def nothing():
        return None

    for c in loads[2:]:
        c.wait()
    for c in halves:
        c.wait_recv()
    experts(0, 32, rr, nothing)
    for c, f in zip(opposite(1), onward(1)):
        c.wait_recv()
        f.start()
    go(direct(1))
    arrived(onward(0) + onward(1) + direct(0))
    experts(32, 64, res, nothing)

    back_opp = [
        remote(21, res.at[pl.ds(32, 32), ra], rela, b_up),
        remote(22, res.at[pl.ds(32, 32), rb], relb, b_dn),
    ]
    back_fw = [
        remote(23, rela, rr.at[pl.ds(96, 32), ra], b_up),
        remote(24, relb, rr.at[pl.ds(96, 32), rb], b_dn),
    ]

    def back(g):
        return [
            remote(25 + g, res.at[r16(4 + 2 * g)], rr.at[r16(2 + g)], b_dn),
            remote(27 + g, res.at[r16(5 + 2 * g)], rr.at[r16(4 + g)], b_up),
        ]

    go(back_opp)
    go(back(0))
    arrived(direct(1))

    def relay():
        for c, f in zip(back_opp, back_fw):
            c.wait_recv()
            f.start()

    experts(96, 32, res, relay)
    go(back(1))
    arrived(back(0) + back_fw + back(1))

    width = cut(D, 512)

    @pl.loop(0, D // width)
    def _(i):
        cols = pl.ds(pl.multiple_of(i * width, LANES), width)
        got = jnp.dot(place, rr[:, cols], preferred_element_type=F32)
        own[:, cols] = got[0:16]
        tb[:, cols] = got[16:64].astype(BF)

    swap = lambda v: pltpu.roll(v, 64, 1)
    cols_s = pl.ds(D, LANES)
    got = jnp.dot(place, rr[:, cols_s], preferred_element_type=F32)
    got = resplit(got + swap(got)).astype(F32)
    own[:, cols_s] = got[0:16]
    tb[:, cols_s] = got[16:64].astype(BF)

    opp_a = remote(29, tb.at[r16(2), ra], add_a, a_up)
    opp_b = remote(30, tb.at[r16(2), rb], add_b, a_dn)
    plain_b = remote(31, tb.at[r16(1), rb], from_m.at[:, rb], a_up)
    plain_a = remote(32, tb.at[r16(0), ra], from_p.at[:, ra], a_dn)
    summed_a = remote(33, fin.at[0, :, ra], from_m.at[:, ra], a_up)
    summed_b = remote(34, fin.at[0, :, rb], from_p.at[:, rb], a_dn)
    go([opp_a, opp_b, plain_b, plain_a])
    opp_a.wait_recv()
    fin[0, :, ra] = (tb[r16(1), ra].astype(F32) + add_a[...].astype(F32)).astype(BF)
    summed_a.start()
    opp_b.wait_recv()
    rm = pl.ds(half, half)
    fin[0, :, rm] = (
        tb[r16(0), rm].astype(F32) + add_b[:, 0:half].astype(F32)
    ).astype(BF)
    got = tb[r16(0), cols_s].astype(F32) + add_b[:, half : half + LANES].astype(F32)
    fin[0, :, cols_s] = resplit(got + swap(got))
    summed_b.start()

    last_a = remote(35, fin.at[1, :, ra], out.at[0, :, ra], z_dn)
    last_b = remote(36, fin.at[1, :, rm], out.at[0, :, rm], z_dn)
    arrived([plain_a, summed_a])
    fin[1, :, ra] = (
        own[:, ra] + from_m[:, ra].astype(F32) + from_p[:, ra].astype(F32)
    ).astype(BF)
    last_a.start()
    arrived([plain_b, summed_b])
    fin[1, :, rm] = (
        own[:, rm] + from_m[:, rm].astype(F32) + from_p[:, rm].astype(F32)
    ).astype(BF)
    last_b.start()
    got = own[:, cols_s] + from_m[:, cols_s].astype(F32) + from_p[:, cols_s].astype(F32)
    got = got + swap(got)
    route[0] = jnp.concatenate(
        [
            jnp.sum(jnp.where(lane16 == ids[:, k : k + 1], got, 0.0), axis=1, keepdims=True)
            for k in range(2)
        ],
        axis=1,
    )

    every = [up_x, up_d, dn_d, dn_x, fw_x, fw_d] + halves
    for g in range(2):
        every = every + direct(g) + opposite(g) + onward(g) + back(g)
    every = every + back_opp + back_fw
    every = every + [opp_a, opp_b, plain_a, plain_b, summed_a, summed_b, last_a, last_b]
    for c in every:
        c.wait_send()
    arrived([last_a, last_b])


def on_device(tokens_in, out_grad, expert_ids, gate_weights, w_gate, w_up, w_down):
    D = tokens_in.shape[2]
    W = w_gate.shape[1]
    wide, back, half = 2 * D + LANES, D + LANES, D // 2
    hbm = pl.BlockSpec(memory_space=pl.ANY)
    vmem = pl.BlockSpec(memory_space=pltpu.VMEM)
    return pl.pallas_call(
        kernel,
        out_shape=(
            jax.ShapeDtypeStruct(tokens_in.shape, BF),
            jax.ShapeDtypeStruct(expert_ids.shape, F32),
        ),
        in_specs=[hbm, hbm, vmem, vmem, hbm, hbm, hbm],
        out_specs=(hbm, vmem),
        scratch_shapes=[
            pltpu.VMEM((64, wide), BF),
            pltpu.VMEM((2, 48, wide), BF),
            pltpu.VMEM((128, wide), BF),
            pltpu.VMEM((2, 16, D), BF),
            pltpu.VMEM((2, 16, D + LANES), BF),
            pltpu.VMEM((4 * W, D), BF),
            pltpu.VMEM((2 * W, D), BF),
            pltpu.VMEM((64, 4 * W), F32),
            pltpu.VMEM((64, 2 * W), F32),
            pltpu.VMEM((128, back), BF),
            pltpu.VMEM((128, back), BF),
            pltpu.VMEM((32, half), BF),
            pltpu.VMEM((32, half + LANES), BF),
            pltpu.VMEM((48, back), BF),
            pltpu.VMEM((16, back), F32),
            pltpu.VMEM((16, back), BF),
            pltpu.VMEM((16, back), BF),
            pltpu.VMEM((16, half), BF),
            pltpu.VMEM((16, half + LANES), BF),
            pltpu.VMEM((2, 16, back), BF),
            pltpu.SemaphoreType.DMA((COPIES,)),
            pltpu.SemaphoreType.DMA((COPIES,)),
            pltpu.SemaphoreType.DMA((5,)),
        ],
        compiler_params=pltpu.CompilerParams(collective_id=0, has_side_effects=True),
    )(tokens_in, out_grad, expert_ids, gate_weights, w_gate, w_up, w_down)


def solution(mesh):
    spec = P("section", "expert", None)
    return jax.shard_map(
        on_device, mesh=mesh, in_specs=(spec,) * 7, out_specs=(spec, spec), check_vma=False
    )
```

```python
import jax
import jax.numpy as jnp
from jax import lax
from jax.experimental import pallas as pl
from jax.experimental.pallas import tpu as pltpu
from jax.sharding import PartitionSpec as P

MESH = pl.DeviceIdType.MESH
BF = jnp.bfloat16
F32 = jnp.float32
NT = (((1,), (1,)), ((), ()))
EXPERTS = 8
Q = 8
LANES = 128
COPIES = 64
PIECES = 4


def iota(shape, dim):
    return lax.broadcasted_iota(jnp.int32, shape, dim)


def ones(mask):
    return mask.astype(F32).astype(BF)


def dot_nt(left, right):
    return lax.dot_general(left, right, NT, preferred_element_type=F32)


def resplit(total):
    high = total.astype(BF).astype(F32)
    lane = iota(total.shape, 1)
    return jnp.where(lane < 64, high, total - high).astype(BF)


def kernel(
    x_in, dy_in, ids_in, gw_in, wg_in, wu_in, wd_in, out, route,
    blk, sel, xin, w1, w2, acc, acd, res, rr, tb, own, parts, fin,
    send, recv, local,
):
    D = x_in.shape[2]
    W = wg_in.shape[1]
    sec = lax.axis_index("section")
    secs = lax.axis_size("section")
    me = lax.axis_index("expert")
    core = me % 2
    y = (me // 2) % 4
    x = me // 8
    first = core * y + (1 - core) * x
    second = core * x + (1 - core) * y
    step_a = 8 - 6 * core
    step_b = 2 + 6 * core

    def at(pos_a, pos_b):
        return (sec, core + step_a * (pos_a % 4) + step_b * (pos_b % 4))

    a_up, a_dn, a_op = [at(first + k, second) for k in (1, 3, 2)]
    b_up, b_dn, b_op = [at(first, second + k) for k in (1, 3, 2)]
    sib = (sec, me + 1 - 2 * core)
    z_dn = ((sec + secs - 1) % secs, me)
    z_up = ((sec + 1) % secs, me)
    own_e = me // 4

    def expert_at(pos_b):
        pos_b = pos_b % 4
        return (1 - core) * (x * 2 + pos_b // 2) + core * (pos_b * 2 + y // 2)

    peers = [expert_at(second + off) for off in (0, 1, 3, 2)]

    flying, landing = {}, {}

    class Push:
        def __init__(self, src, dst, dev):
            self.i = Push.count
            Push.count += 1
            self.copy = pltpu.make_async_remote_copy(
                src_ref=src, dst_ref=dst, send_sem=send.at[self.i],
                recv_sem=recv.at[self.i], device_id=dev, device_id_type=MESH,
            )

        def start(self):
            self.copy.start()
            flying[self.i] = landing[self.i] = self.copy

        def wait(self):
            self.copy.wait_recv()
            landing.pop(self.i)

    Push.count = 0

    def go(copies):
        for c in copies:
            c.start()

    def arrived(copies):
        for c in copies:
            c.wait()

    def finish():
        for c in landing.values():
            c.wait_recv()
        for c in flying.values():
            c.wait_send()

    r16 = lambda i: pl.ds(16 * i, 16)
    side = pl.ds(D, LANES)
    step = D // PIECES
    piece = [
        pl.ds(i * step, step + (LANES if i == PIECES - 1 else 0)) for i in range(PIECES)
    ]

    loads = [
        pltpu.make_async_copy(s, d, local.at[i])
        for i, (s, d) in enumerate(
            [
                (x_in.at[0], blk.at[r16(0), pl.ds(0, D)]),
                (dy_in.at[0], blk.at[r16(0), pl.ds(D, D)]),
                (wg_in.at[0], w1.at[pl.ds(0, W)]),
                (wu_in.at[0], w1.at[pl.ds(2 * W, W)]),
                (wd_in.at[0], w2.at[pl.ds(0, W)]),
            ]
        )
    ]
    for c in loads:
        c.start()

    barrier = pltpu.get_barrier_semaphore()
    around = (a_up, a_dn, a_op, b_up, b_dn, b_op, sib, z_dn, z_up)
    for dev in around:
        pl.semaphore_signal(barrier, inc=1, device_id=dev, device_id_type=MESH)

    ids = ids_in[0]
    gates = gw_in[0].astype(F32)
    eye = ones(iota((16, 16), 0) == iota((16, 16), 1))
    row_e = iota((LANES, 16), 0)
    table = jnp.zeros((LANES, 16), F32)
    for k in range(2):
        table = table + jnp.where(row_e == ids[k : k + 1], gates[k : k + 1], 0.0)
    blk[r16(0), pl.ds(2 * D, LANES)] = dot_nt(eye, table.astype(BF)).astype(BF)

    pl.semaphore_wait(barrier, len(around))
    loads[0].wait()
    loads[1].wait()

    gather = [
        Push(blk.at[r16(0)], blk.at[r16(q)], dev)
        for q, dev in ((1, a_up), (2, a_dn), (3, a_op))
    ]
    go(gather)
    halves = [
        Push(wg_in.at[0], w1.at[pl.ds(W, W)], sib),
        Push(wu_in.at[0], w1.at[pl.ds(3 * W, W)], sib),
        Push(wd_in.at[0], w2.at[pl.ds(W, W)], sib),
    ]
    go(halves)

    def of_peer(index):
        e = jnp.full(index.shape, peers[3], jnp.int32)
        for j in (2, 1, 0):
            e = jnp.where(index == j, peers[j], e)
        return e

    def cut(size, want):
        return max(d for d in range(LANES, want + 1, LANES) if size % d == 0)

    r32, c32 = iota((32, 32), 0), iota((32, 32), 1)
    lower = ones((r32 // 16 == c32 // 16) & (c32 < r32))
    pick = ones(iota((64, LANES), 1) == of_peer(iota((64, LANES), 0) // 16))

    def routing(g):
        hit = ones(blk[pl.ds(32 * g, 32), pl.ds(2 * D, LANES)].astype(F32) > 0.0)
        return hit, jnp.dot(lower, hit, preferred_element_type=F32).astype(BF)

    def select(g):
        hit, rank = routing(g)
        r, c = iota((64, 32), 0), iota((64, 32), 1)
        good = (dot_nt(pick, hit) > 0.5) & (dot_nt(pick, rank) == (r % 8).astype(F32))
        perm = ones(good & ((r // 8) % 2 == c // 16))
        width = cut(2 * D + LANES, 1664)

        @pl.loop(0, (2 * D + LANES) // width)
        def _(i):
            cols = pl.ds(pl.multiple_of(i * width, LANES), width)
            got = jnp.dot(
                perm, blk[pl.ds(32 * g, 32), cols], preferred_element_type=F32
            ).astype(BF)
            xin[r16(4 * g), cols] = got[0:16]
            sel[g, :, cols] = got[16:64]

    def placing(g):
        hit, rank = routing(g)
        r, c = iota((32, 64), 0), iota((32, 64), 1)
        good = (dot_nt(hit, pick) > 0.5) & (dot_nt(rank, pick) == (c % 8).astype(F32))
        return ones(good & ((c // 8) % 2 == r // 16))

    def dispatch(g):
        return [
            [
                Push(sel.at[g, r16(j - 1), cols], xin.at[r16(4 * g + j), cols], dev)
                for j, dev in ((3, b_op), (1, b_up), (2, b_dn))
            ]
            for cols in (pl.ds(0, D), pl.ds(D, D + LANES))
        ]

    sent = [dispatch(0), dispatch(1)]
    back = [
        [
            [
                Push(res.at[g, r16(j - 1), cols], rr.at[r16(4 * g + j), cols], dev)
                for j, dev in ((3, b_op), (1, b_dn), (2, b_up))
            ]
            for cols in piece
        ]
        for g in range(2)
    ]
    reduce = {
        q: [Push(tb.at[r16(q - 1), cols], parts.at[q - 1, :, cols], dev) for cols in piece]
        for q, dev in ((1, a_dn), (2, a_up), (3, a_op))
    }
    last = [
        Push(fin.at[:, pl.ds(i * step, step)], out.at[0, :, pl.ds(i * step, step)], z_dn)
        for i in range(PIECES)
    ]

    gather[0].wait()
    select(0)
    go(sent[0][0] + sent[0][1])
    arrived(gather[1:])
    select(1)
    go(sent[1][0] + sent[1][1])
    place = [placing(0), placing(1)]

    for c in loads[2:]:
        c.wait()
    arrived(halves)
    depth = 512 if D % 512 == 0 else LANES

    def experts(g):
        rows = pl.ds(64 * g, 64)
        acc[...] = jnp.zeros((64, 4 * W), F32)
        acd[...] = jnp.zeros((64, 2 * W), F32)
        arrived(sent[g][0])

        @pl.loop(0, D // depth)
        def _(k):
            cols = pl.ds(pl.multiple_of(k * depth, LANES), depth)
            acc[...] += dot_nt(xin[rows, cols], w1[:, cols])

        arrived(sent[g][1])

        @pl.loop(0, D // depth)
        def _(k):
            cols = pl.ds(pl.multiple_of(k * depth, LANES), depth)
            cols_d = pl.ds(pl.multiple_of(D + k * depth, LANES), depth)
            acd[...] += dot_nt(xin[rows, cols_d], w2[:, cols])

        gate_pre = acc[:, 0 : 2 * W]
        up_pre = acc[:, 2 * W : 4 * W]
        hidden = acd[...]
        lane = iota((64, LANES), 1)
        gate = jnp.sum(
            jnp.where(lane == own_e, xin[rows, pl.ds(2 * D, LANES)].astype(F32), 0.0),
            axis=1, keepdims=True,
        )
        sig = jax.nn.sigmoid(gate_pre)
        act = gate_pre * sig
        slope = sig * (1.0 + gate_pre * (1.0 - sig))
        score = jnp.sum(act * up_pre * hidden, axis=1, keepdims=True)
        scaled = hidden * gate
        grads = jnp.concatenate(
            [(scaled * up_pre * slope).astype(BF), (scaled * act).astype(BF)], axis=1
        )
        scores = resplit(jnp.where((lane % 64) == own_e, score, 0.0))
        rr[r16(4 * g), side] = scores[0:16]
        res[g, :, side] = scores[16:64]
        width = cut(step, 512)
        for i in range(PIECES):

            @pl.loop(0, step // width)
            def _(k):
                cols = pl.ds(pl.multiple_of(i * step + k * width, LANES), width)
                got = jnp.dot(
                    grads, w1[:, cols], preferred_element_type=F32
                ).astype(BF)
                rr[r16(4 * g), cols] = got[0:16]
                res[g, :, cols] = got[16:64]

            go(back[g][i])

    experts(0)
    experts(1)

    swap = lambda v: pltpu.roll(v, 64, 1)
    for g in range(2):
        rows = pl.ds(64 * g, 64)
        for i in range(PIECES):
            arrived(back[g][i])
            cols = pl.ds(i * step, step)
            got = jnp.dot(place[g], rr[rows, cols], preferred_element_type=F32)
            got_s = None
            if i == PIECES - 1:
                got_s = jnp.dot(place[g], rr[rows, side], preferred_element_type=F32)
                got_s = resplit(got_s + swap(got_s))
            if g == 0:
                own[:, cols] = got[0:16]
                tb[r16(0), cols] = got[16:32].astype(BF)
                if got_s is not None:
                    own[:, side] = got_s[0:16].astype(F32)
                    tb[r16(0), side] = got_s[16:32]
                go([reduce[1][i]])
            else:
                tb[pl.ds(16, 32), cols] = got.astype(BF)
                if got_s is not None:
                    tb[pl.ds(16, 32), side] = got_s
                go([reduce[3][i], reduce[2][i]])

    def total(cols):
        got = own[:, cols]
        for q in range(3):
            got = got + parts[q, :, cols].astype(F32)
        return got

    for i in range(PIECES):
        arrived([reduce[q][i] for q in (1, 2, 3)])
        cols = pl.ds(i * step, step)
        fin[:, cols] = total(cols).astype(BF)
        last[i].start()

    got = total(side)
    got = got + swap(got)
    ids_col = dot_nt(eye, ids.astype(F32).astype(BF))
    lane16 = iota((16, LANES), 1).astype(F32)
    for k in range(2):
        col = jnp.sum(
            jnp.where(lane16 == ids_col[:, k : k + 1], got, 0.0), axis=1, keepdims=True
        )
        route[0, k : k + 1, :] = jnp.sum(
            jnp.where(iota((16, 16), 0) == iota((16, 16), 1), col, 0.0),
            axis=0, keepdims=True,
        )
    finish()


def on_device(tokens_in, out_grad, expert_ids, gate_weights, w_gate, w_up, w_down):
    D = tokens_in.shape[2]
    W = w_gate.shape[1]
    wide, back = 2 * D + LANES, D + LANES
    hbm = pl.BlockSpec(memory_space=pl.ANY)
    vmem = pl.BlockSpec(memory_space=pltpu.VMEM)
    ids = jnp.swapaxes(expert_ids, 1, 2)
    grad, route = pl.pallas_call(
        kernel,
        out_shape=(
            jax.ShapeDtypeStruct(tokens_in.shape, BF),
            jax.ShapeDtypeStruct(ids.shape, F32),
        ),
        in_specs=[hbm, hbm, vmem, vmem, hbm, hbm, hbm],
        out_specs=(hbm, vmem),
        scratch_shapes=[
            pltpu.VMEM((64, wide), BF),
            pltpu.VMEM((2, 48, wide), BF),
            pltpu.VMEM((128, wide), BF),
            pltpu.VMEM((4 * W, D), BF),
            pltpu.VMEM((2 * W, D), BF),
            pltpu.VMEM((64, 4 * W), F32),
            pltpu.VMEM((64, 2 * W), F32),
            pltpu.VMEM((2, 48, back), BF),
            pltpu.VMEM((128, back), BF),
            pltpu.VMEM((48, back), BF),
            pltpu.VMEM((16, back), F32),
            pltpu.VMEM((3, 16, back), BF),
            pltpu.VMEM((16, D), BF),
            pltpu.SemaphoreType.DMA((COPIES,)),
            pltpu.SemaphoreType.DMA((COPIES,)),
            pltpu.SemaphoreType.DMA((5,)),
        ],
        compiler_params=pltpu.CompilerParams(collective_id=0, has_side_effects=True),
    )(tokens_in, out_grad, ids, jnp.swapaxes(gate_weights, 1, 2), w_gate, w_up, w_down)
    return grad, jnp.swapaxes(route, 1, 2)


def solution(mesh):
    spec = P("section", "expert", None)
    return jax.shard_map(
        on_device, mesh=mesh, in_specs=(spec,) * 7, out_specs=(spec, spec), check_vma=False
    )
```

```python
import jax
import jax.numpy as jnp
from jax import lax
from jax.experimental import pallas as pl
from jax.experimental.pallas import tpu as pltpu
from jax.sharding import PartitionSpec as P

MESH = pl.DeviceIdType.MESH
BF = jnp.bfloat16
F32 = jnp.float32
NT = (((1,), (1,)), ((), ()))
EXPERTS = 8
Q = 8
LANES = 128
COPIES = 64
PIECES = 4


def iota(shape, dim):
    return lax.broadcasted_iota(jnp.int32, shape, dim)


def ones(mask):
    return mask.astype(F32).astype(BF)


def dot_nt(left, right):
    return lax.dot_general(left, right, NT, preferred_element_type=F32)


def resplit(total):
    high = total.astype(BF).astype(F32)
    lane = iota(total.shape, 1)
    return jnp.where(lane < 64, high, total - high).astype(BF)


def kernel(
    x_in, dy_in, ids_in, gw_in, wg_in, wu_in, wd_in, out, route,
    blk, sel, xin, w1, w2, acc, res, rr, tb, own, parts, fin,
    send, recv, local,
):
    D = x_in.shape[2]
    W = wg_in.shape[1]
    sec = lax.axis_index("section")
    secs = lax.axis_size("section")
    me = lax.axis_index("expert")
    core = me % 2
    y = (me // 2) % 4
    x = me // 8
    first = core * y + (1 - core) * x
    second = core * x + (1 - core) * y
    step_a = 8 - 6 * core
    step_b = 2 + 6 * core

    def at(pos_a, pos_b):
        return (sec, core + step_a * (pos_a % 4) + step_b * (pos_b % 4))

    a_up, a_dn, a_op = [at(first + k, second) for k in (1, 3, 2)]
    b_up, b_dn, b_op = [at(first, second + k) for k in (1, 3, 2)]
    sib = (sec, me + 1 - 2 * core)
    z_dn = ((sec + secs - 1) % secs, me)
    z_up = ((sec + 1) % secs, me)
    own_e = me // 4

    def expert_at(pos_b):
        pos_b = pos_b % 4
        return (1 - core) * (x * 2 + pos_b // 2) + core * (pos_b * 2 + y // 2)

    peers = [expert_at(second + off) for off in (0, 1, 3, 2)]

    flying, landing = {}, {}

    class Push:
        def __init__(self, src, dst, dev):
            self.i = Push.count
            Push.count += 1
            self.copy = pltpu.make_async_remote_copy(
                src_ref=src, dst_ref=dst, send_sem=send.at[self.i],
                recv_sem=recv.at[self.i], device_id=dev, device_id_type=MESH,
            )

        def start(self):
            self.copy.start()
            flying[self.i] = landing[self.i] = self.copy

        def wait(self):
            self.copy.wait_recv()
            landing.pop(self.i)

    Push.count = 0

    def go(copies):
        for c in copies:
            c.start()

    def arrived(copies):
        for c in copies:
            c.wait()

    def finish():
        for c in landing.values():
            c.wait_recv()
        for c in flying.values():
            c.wait_send()

    r16 = lambda i: pl.ds(16 * i, 16)
    side = pl.ds(D, LANES)
    head = pl.ds(0, LANES)
    parts_in = (pl.ds(0, LANES + D), pl.ds(LANES + D, D))
    step = D // PIECES
    piece = [
        pl.ds(i * step, step + (LANES if i == PIECES - 1 else 0)) for i in range(PIECES)
    ]

    loads = [
        pltpu.make_async_copy(s, d, local.at[i])
        for i, (s, d) in enumerate(
            [
                (x_in.at[0], blk.at[r16(0), pl.ds(LANES, D)]),
                (dy_in.at[0], blk.at[r16(0), pl.ds(LANES + D, D)]),
                (wg_in.at[0], w1.at[pl.ds(0, W)]),
                (wu_in.at[0], w1.at[pl.ds(2 * W, W)]),
                (wd_in.at[0], w2.at[pl.ds(0, W)]),
            ]
        )
    ]
    for c in loads:
        c.start()

    barrier = pltpu.get_barrier_semaphore()
    around = (a_up, a_dn, a_op, b_up, b_dn, b_op, sib, z_dn, z_up)
    for dev in around:
        pl.semaphore_signal(barrier, inc=1, device_id=dev, device_id_type=MESH)

    ids = ids_in[0]
    gates = gw_in[0].astype(F32)
    eye = ones(iota((16, 16), 0) == iota((16, 16), 1))
    row_e = iota((LANES, 16), 0)
    table = jnp.zeros((LANES, 16), F32)
    for k in range(2):
        table = table + jnp.where(row_e == ids[k : k + 1], gates[k : k + 1], 0.0)
    blk[r16(0), head] = dot_nt(eye, table.astype(BF)).astype(BF)

    pl.semaphore_wait(barrier, len(around))
    loads[0].wait()

    gather = [
        [
            Push(blk.at[r16(0), cols], blk.at[r16(q), cols], dev)
            for q, dev in ((1, a_up), (2, a_dn), (3, a_op))
        ]
        for cols in parts_in
    ]
    go(gather[0][:2])
    loads[1].wait()
    go(gather[1][:2] + [gather[0][2], gather[1][2]])
    halves = [
        Push(wg_in.at[0], w1.at[pl.ds(W, W)], sib),
        Push(wu_in.at[0], w1.at[pl.ds(3 * W, W)], sib),
        Push(wd_in.at[0], w2.at[pl.ds(W, W)], sib),
    ]
    go(halves)

    def of_peer(index):
        e = jnp.full(index.shape, peers[3], jnp.int32)
        for j in (2, 1, 0):
            e = jnp.where(index == j, peers[j], e)
        return e

    def cut(size, want):
        return max(d for d in range(LANES, want + 1, LANES) if size % d == 0)

    r32, c32 = iota((32, 32), 0), iota((32, 32), 1)
    lower = ones((r32 // 16 == c32 // 16) & (c32 < r32))
    pick = ones(iota((64, LANES), 1) == of_peer(iota((64, LANES), 0) // 16))

    def routing(g):
        hit = ones(blk[pl.ds(32 * g, 32), head].astype(F32) > 0.0)
        return hit, jnp.dot(lower, hit, preferred_element_type=F32).astype(BF)

    def selection(g):
        hit, rank = routing(g)
        r, c = iota((64, 32), 0), iota((64, 32), 1)
        good = (dot_nt(pick, hit) > 0.5) & (dot_nt(pick, rank) == (r % 8).astype(F32))
        return ones(good & ((r // 8) % 2 == c // 16))

    def select(g, perm, part):
        start, size = part.start, part.size
        width = cut(size, 1408)

        @pl.loop(0, size // width)
        def _(i):
            cols = pl.ds(pl.multiple_of(start + i * width, LANES), width)
            got = jnp.dot(
                perm, blk[pl.ds(32 * g, 32), cols], preferred_element_type=F32
            ).astype(BF)
            xin[r16(4 * g), cols] = got[0:16]
            sel[g, :, cols] = got[16:64]

    def placing(g):
        hit, rank = routing(g)
        r, c = iota((32, 64), 0), iota((32, 64), 1)
        good = (dot_nt(hit, pick) > 0.5) & (dot_nt(rank, pick) == (c % 8).astype(F32))
        return ones(good & ((c // 8) % 2 == r // 16))

    def dispatch(g):
        return [
            [
                Push(sel.at[g, r16(j - 1), cols], xin.at[r16(4 * g + j), cols], dev)
                for j, dev in ((3, b_op), (1, b_up), (2, b_dn))
            ]
            for cols in parts_in
        ]

    sent = [dispatch(0), dispatch(1)]
    back = [
        [
            [
                Push(res.at[g, r16(j - 1), cols], rr.at[r16(4 * g + j), cols], dev)
                for j, dev in ((3, b_op), (1, b_dn), (2, b_up))
            ]
            for cols in piece
        ]
        for g in range(2)
    ]
    reduce = {
        q: [Push(tb.at[r16(q - 1), cols], parts.at[q - 1, :, cols], dev) for cols in piece]
        for q, dev in ((1, a_dn), (2, a_up), (3, a_op))
    }
    last = [
        Push(fin.at[:, pl.ds(i * step, step)], out.at[0, :, pl.ds(i * step, step)], z_dn)
        for i in range(PIECES)
    ]

    for g in range(2):
        mine = (lambda k: [gather[k][0]]) if g == 0 else (lambda k: gather[k][1:])
        arrived(mine(0))
        perm = selection(g)
        select(g, perm, parts_in[0])
        go(sent[g][0])
        arrived(mine(1))
        select(g, perm, parts_in[1])
        go(sent[g][1])
    place = [placing(0), placing(1)]

    for c in loads[2:]:
        c.wait()
    arrived(halves)
    tall = 2 * W

    def experts(g):
        rows = pl.ds(64 * g, 64)
        arrived(sent[g][0])

        @pl.loop(0, 2)
        def _(k):
            units = pl.ds(pl.multiple_of(k * tall, tall), tall)
            acc[units] = dot_nt(w1[units], xin[rows, pl.ds(LANES, D)])

        arrived(sent[g][1])
        hidden = dot_nt(w2[...], xin[rows, pl.ds(LANES + D, D)])
        gate_pre = acc[0:tall]
        up_pre = acc[tall : 2 * tall]
        chosen = ones(iota((16, LANES), 1) == own_e)
        gate = dot_nt(chosen, xin[rows, head])[0:1]
        sig = jax.nn.sigmoid(gate_pre)
        act = gate_pre * sig
        slope = sig * (1.0 + gate_pre * (1.0 - sig))
        score = jnp.sum(act * up_pre * hidden, axis=0, keepdims=True)
        scaled = hidden * gate
        grads = jnp.concatenate(
            [
                jnp.transpose(scaled * up_pre * slope).astype(BF),
                jnp.transpose(scaled * act).astype(BF),
            ],
            axis=1,
        )
        score = jnp.sum(
            jnp.where(iota((64, 64), 0) == iota((64, 64), 1), score, 0.0),
            axis=1, keepdims=True,
        )
        lane = iota((64, LANES), 1)
        scores = resplit(jnp.where((lane % 64) == own_e, score, 0.0))
        rr[r16(4 * g), side] = scores[0:16]
        res[g, :, side] = scores[16:64]
        width = cut(step, 512)
        for i in range(PIECES):

            @pl.loop(0, step // width)
            def _(k):
                cols = pl.ds(pl.multiple_of(i * step + k * width, LANES), width)
                got = jnp.dot(
                    grads, w1[:, cols], preferred_element_type=F32
                ).astype(BF)
                rr[r16(4 * g), cols] = got[0:16]
                res[g, :, cols] = got[16:64]

            go(back[g][i])

    experts(0)
    experts(1)

    swap = lambda v: pltpu.roll(v, 64, 1)
    for g in range(2):
        rows = pl.ds(64 * g, 64)
        for i in range(PIECES):
            arrived(back[g][i])
            cols = pl.ds(i * step, step)
            got = jnp.dot(place[g], rr[rows, cols], preferred_element_type=F32)
            got_s = None
            if i == PIECES - 1:
                got_s = jnp.dot(place[g], rr[rows, side], preferred_element_type=F32)
                got_s = resplit(got_s + swap(got_s))
            if g == 0:
                own[:, cols] = got[0:16]
                tb[r16(0), cols] = got[16:32].astype(BF)
                if got_s is not None:
                    own[:, side] = got_s[0:16].astype(F32)
                    tb[r16(0), side] = got_s[16:32]
                go([reduce[1][i]])
            else:
                tb[pl.ds(16, 32), cols] = got.astype(BF)
                if got_s is not None:
                    tb[pl.ds(16, 32), side] = got_s
                go([reduce[3][i], reduce[2][i]])

    def total(cols):
        got = own[:, cols]
        for q in range(3):
            got = got + parts[q, :, cols].astype(F32)
        return got

    for i in range(PIECES):
        arrived([reduce[q][i] for q in (1, 2, 3)])
        cols = pl.ds(i * step, step)
        fin[:, cols] = total(cols).astype(BF)
        last[i].start()

    got = total(side)
    got = got + swap(got)
    ids_col = dot_nt(eye, ids.astype(F32).astype(BF))
    lane16 = iota((16, LANES), 1).astype(F32)
    for k in range(2):
        col = jnp.sum(
            jnp.where(lane16 == ids_col[:, k : k + 1], got, 0.0), axis=1, keepdims=True
        )
        route[0, k : k + 1, :] = jnp.sum(
            jnp.where(iota((16, 16), 0) == iota((16, 16), 1), col, 0.0),
            axis=0, keepdims=True,
        )
    finish()


def on_device(tokens_in, out_grad, expert_ids, gate_weights, w_gate, w_up, w_down):
    D = tokens_in.shape[2]
    W = w_gate.shape[1]
    wide, back = 2 * D + LANES, D + LANES
    hbm = pl.BlockSpec(memory_space=pl.ANY)
    vmem = pl.BlockSpec(memory_space=pltpu.VMEM)
    ids = jnp.swapaxes(expert_ids, 1, 2)
    grad, route = pl.pallas_call(
        kernel,
        out_shape=(
            jax.ShapeDtypeStruct(tokens_in.shape, BF),
            jax.ShapeDtypeStruct(ids.shape, F32),
        ),
        in_specs=[hbm, hbm, vmem, vmem, hbm, hbm, hbm],
        out_specs=(hbm, vmem),
        scratch_shapes=[
            pltpu.VMEM((64, wide), BF),
            pltpu.VMEM((2, 48, wide), BF),
            pltpu.VMEM((128, wide), BF),
            pltpu.VMEM((4 * W, D), BF),
            pltpu.VMEM((2 * W, D), BF),
            pltpu.VMEM((4 * W, 64), F32),
            pltpu.VMEM((2, 48, back), BF),
            pltpu.VMEM((128, back), BF),
            pltpu.VMEM((48, back), BF),
            pltpu.VMEM((16, back), F32),
            pltpu.VMEM((3, 16, back), BF),
            pltpu.VMEM((16, D), BF),
            pltpu.SemaphoreType.DMA((COPIES,)),
            pltpu.SemaphoreType.DMA((COPIES,)),
            pltpu.SemaphoreType.DMA((5,)),
        ],
        compiler_params=pltpu.CompilerParams(collective_id=0, has_side_effects=True),
    )(tokens_in, out_grad, ids, jnp.swapaxes(gate_weights, 1, 2), w_gate, w_up, w_down)
    return grad, jnp.swapaxes(route, 1, 2)


def solution(mesh):
    spec = P("section", "expert", None)
    return jax.shard_map(
        on_device, mesh=mesh, in_specs=(spec,) * 7, out_specs=(spec, spec), check_vma=False
    )
```

```python
import jax
import jax.numpy as jnp
from jax import lax
from jax.experimental import pallas as pl
from jax.experimental.pallas import tpu as pltpu
from jax.sharding import PartitionSpec as P

MESH = pl.DeviceIdType.MESH
BF = jnp.bfloat16
F32 = jnp.float32
NT = (((1,), (1,)), ((), ()))
EXPERTS = 8
Q = 8
LANES = 128
COPIES = 64
PIECES = 4


def iota(shape, dim):
    return lax.broadcasted_iota(jnp.int32, shape, dim)


def ones(mask):
    return mask.astype(F32).astype(BF)


def dot_nt(left, right):
    return lax.dot_general(left, right, NT, preferred_element_type=F32)


def resplit(total):
    high = total.astype(BF).astype(F32)
    lane = iota(total.shape, 1)
    return jnp.where(lane < 64, high, total - high).astype(BF)


def kernel(
    x_in, dy_in, ids_in, gw_in, wg_in, wu_in, wd_in, out, route,
    blk, sel, xin, w1, w2, acc, res, rr, tb, own, parts, fin,
    ids_v, gates_v, route_v, send, recv, local,
):
    D = x_in.shape[2]
    W = wg_in.shape[1]
    sec = lax.axis_index("section")
    secs = lax.axis_size("section")
    me = lax.axis_index("expert")
    core = me % 2
    y = (me // 2) % 4
    x = me // 8
    first = core * y + (1 - core) * x
    second = core * x + (1 - core) * y
    step_a = 8 - 6 * core
    step_b = 2 + 6 * core

    def at(pos_a, pos_b):
        return (sec, core + step_a * (pos_a % 4) + step_b * (pos_b % 4))

    a_up, a_dn, a_op = [at(first + k, second) for k in (1, 3, 2)]
    b_up, b_dn, b_op = [at(first, second + k) for k in (1, 3, 2)]
    sib = (sec, me + 1 - 2 * core)
    z_dn = ((sec + secs - 1) % secs, me)
    z_up = ((sec + 1) % secs, me)
    own_e = me // 4

    def expert_at(pos_b):
        pos_b = pos_b % 4
        return (1 - core) * (x * 2 + pos_b // 2) + core * (pos_b * 2 + y // 2)

    peers = [expert_at(second + off) for off in (0, 1, 3, 2)]

    flying, landing = {}, {}

    class Push:
        def __init__(self, src, dst, dev):
            self.i = Push.count
            Push.count += 1
            self.copy = pltpu.make_async_remote_copy(
                src_ref=src, dst_ref=dst, send_sem=send.at[self.i],
                recv_sem=recv.at[self.i], device_id=dev, device_id_type=MESH,
            )

        def start(self):
            self.copy.start()
            flying[self.i] = landing[self.i] = self.copy

        def wait(self):
            self.copy.wait_recv()
            landing.pop(self.i)

    Push.count = 0

    def go(copies):
        for c in copies:
            c.start()

    def arrived(copies):
        for c in copies:
            c.wait()

    def finish():
        for c in landing.values():
            c.wait_recv()
        for c in flying.values():
            c.wait_send()

    r16 = lambda i: pl.ds(16 * i, 16)
    side = pl.ds(D, LANES)
    head = pl.ds(0, LANES)
    parts_in = (pl.ds(0, LANES + D), pl.ds(LANES + D, D))
    step = D // PIECES
    piece = [
        pl.ds(i * step, step + (LANES if i == PIECES - 1 else 0)) for i in range(PIECES)
    ]

    barrier = pltpu.get_barrier_semaphore()
    around = (a_up, a_dn, a_op, b_up, b_dn, b_op, sib, z_dn, z_up)
    for dev in around:
        pl.semaphore_signal(barrier, inc=1, device_id=dev, device_id_type=MESH)

    loads = [
        pltpu.make_async_copy(s, d, local.at[i])
        for i, (s, d) in enumerate(
            [
                (ids_in.at[0], ids_v),
                (gw_in.at[0], gates_v),
                (x_in.at[0], blk.at[r16(0), pl.ds(LANES, D)]),
                (dy_in.at[0], blk.at[r16(0), pl.ds(LANES + D, D)]),
                (wg_in.at[0], w1.at[pl.ds(0, W)]),
                (wu_in.at[0], w1.at[pl.ds(2 * W, W)]),
                (wd_in.at[0], w2.at[pl.ds(0, W)]),
            ]
        )
    ]
    for c in loads:
        c.start()

    loads[0].wait()
    loads[1].wait()
    ids = ids_v[...]
    gates = gates_v[...].astype(F32)
    eye = ones(iota((16, 16), 0) == iota((16, 16), 1))
    row_e = iota((LANES, 16), 0)
    table = jnp.zeros((LANES, 16), F32)
    for k in range(2):
        table = table + jnp.where(row_e == ids[k : k + 1], gates[k : k + 1], 0.0)
    blk[r16(0), head] = dot_nt(eye, table.astype(BF)).astype(BF)

    pl.semaphore_wait(barrier, len(around))
    loads[2].wait()

    gather = [
        [
            Push(blk.at[r16(0), cols], blk.at[r16(q), cols], dev)
            for q, dev in ((1, a_up), (2, a_dn), (3, a_op))
        ]
        for cols in parts_in
    ]
    go(gather[0][:2])
    loads[3].wait()
    go(gather[1][:2] + [gather[0][2], gather[1][2]])
    halves = [
        Push(wg_in.at[0], w1.at[pl.ds(W, W)], sib),
        Push(wu_in.at[0], w1.at[pl.ds(3 * W, W)], sib),
        Push(wd_in.at[0], w2.at[pl.ds(W, W)], sib),
    ]
    go(halves)

    def of_peer(index):
        e = jnp.full(index.shape, peers[3], jnp.int32)
        for j in (2, 1, 0):
            e = jnp.where(index == j, peers[j], e)
        return e

    def cut(size, want):
        return max(d for d in range(LANES, want + 1, LANES) if size % d == 0)

    r32, c32 = iota((32, 32), 0), iota((32, 32), 1)
    lower = ones((r32 // 16 == c32 // 16) & (c32 < r32))
    pick = ones(iota((64, LANES), 1) == of_peer(iota((64, LANES), 0) // 16))

    def routing(g):
        hit = ones(blk[pl.ds(32 * g, 32), head].astype(F32) > 0.0)
        return hit, jnp.dot(lower, hit, preferred_element_type=F32).astype(BF)

    def selection(g):
        hit, rank = routing(g)
        r, c = iota((64, 32), 0), iota((64, 32), 1)
        good = (dot_nt(pick, hit) > 0.5) & (dot_nt(pick, rank) == (r % 8).astype(F32))
        return ones(good & ((r // 8) % 2 == c // 16))

    def select(g, perm, part):
        start, size = part.start, part.size
        width = cut(size, 1408)

        @pl.loop(0, size // width)
        def _(i):
            cols = pl.ds(pl.multiple_of(start + i * width, LANES), width)
            got = jnp.dot(
                perm, blk[pl.ds(32 * g, 32), cols], preferred_element_type=F32
            ).astype(BF)
            xin[r16(4 * g), cols] = got[0:16]
            sel[g, :, cols] = got[16:64]

    def placing(g):
        hit, rank = routing(g)
        r, c = iota((32, 64), 0), iota((32, 64), 1)
        good = (dot_nt(hit, pick) > 0.5) & (dot_nt(rank, pick) == (c % 8).astype(F32))
        return ones(good & ((c // 8) % 2 == r // 16))

    def dispatch(g):
        return [
            [
                Push(sel.at[g, r16(j - 1), cols], xin.at[r16(4 * g + j), cols], dev)
                for j, dev in ((3, b_op), (1, b_up), (2, b_dn))
            ]
            for cols in parts_in
        ]

    sent = [dispatch(0), dispatch(1)]
    back = [
        [
            [
                Push(res.at[g, r16(j - 1), cols], rr.at[r16(4 * g + j), cols], dev)
                for j, dev in ((3, b_op), (1, b_dn), (2, b_up))
            ]
            for cols in piece
        ]
        for g in range(2)
    ]
    reduce = {
        q: [Push(tb.at[r16(q - 1), cols], parts.at[q - 1, :, cols], dev) for cols in piece]
        for q, dev in ((1, a_dn), (2, a_up), (3, a_op))
    }
    last = [
        Push(fin.at[:, pl.ds(i * step, step)], out.at[0, :, pl.ds(i * step, step)], z_dn)
        for i in range(PIECES)
    ]

    for g in range(2):
        mine = (lambda k: [gather[k][0]]) if g == 0 else (lambda k: gather[k][1:])
        arrived(mine(0))
        perm = selection(g)
        select(g, perm, parts_in[0])
        go(sent[g][0])
        arrived(mine(1))
        select(g, perm, parts_in[1])
        go(sent[g][1])
    place = [placing(0), placing(1)]

    for c in loads[4:]:
        c.wait()
    arrived(halves)
    tall = 2 * W

    def experts(g):
        rows = pl.ds(64 * g, 64)
        arrived(sent[g][0])

        @pl.loop(0, 2)
        def _(k):
            units = pl.ds(pl.multiple_of(k * tall, tall), tall)
            acc[units] = dot_nt(w1[units], xin[rows, pl.ds(LANES, D)])

        arrived(sent[g][1])
        hidden = dot_nt(w2[...], xin[rows, pl.ds(LANES + D, D)])
        gate_pre = acc[0:tall]
        up_pre = acc[tall : 2 * tall]
        chosen = ones(iota((16, LANES), 1) == own_e)
        gate = dot_nt(chosen, xin[rows, head])[0:1]
        sig = jax.nn.sigmoid(gate_pre)
        act = gate_pre * sig
        slope = sig * (1.0 + gate_pre * (1.0 - sig))
        score = jnp.sum(act * up_pre * hidden, axis=0, keepdims=True)
        scaled = hidden * gate
        grads = jnp.concatenate(
            [
                jnp.transpose(scaled * up_pre * slope).astype(BF),
                jnp.transpose(scaled * act).astype(BF),
            ],
            axis=1,
        )
        score = jnp.sum(
            jnp.where(iota((64, 64), 0) == iota((64, 64), 1), score, 0.0),
            axis=1, keepdims=True,
        )
        lane = iota((64, LANES), 1)
        scores = resplit(jnp.where((lane % 64) == own_e, score, 0.0))
        rr[r16(4 * g), side] = scores[0:16]
        res[g, :, side] = scores[16:64]
        width = cut(step, 512)
        for i in range(PIECES):

            @pl.loop(0, step // width)
            def _(k):
                cols = pl.ds(pl.multiple_of(i * step + k * width, LANES), width)
                got = jnp.dot(
                    grads, w1[:, cols], preferred_element_type=F32
                ).astype(BF)
                rr[r16(4 * g), cols] = got[0:16]
                res[g, :, cols] = got[16:64]

            go(back[g][i])

    experts(0)
    experts(1)

    swap = lambda v: pltpu.roll(v, 64, 1)
    for g in range(2):
        rows = pl.ds(64 * g, 64)
        for i in range(PIECES):
            arrived(back[g][i])
            cols = pl.ds(i * step, step)
            got = jnp.dot(place[g], rr[rows, cols], preferred_element_type=F32)
            got_s = None
            if i == PIECES - 1:
                got_s = jnp.dot(place[g], rr[rows, side], preferred_element_type=F32)
                got_s = resplit(got_s + swap(got_s))
            if g == 0:
                own[:, cols] = got[0:16]
                tb[r16(0), cols] = got[16:32].astype(BF)
                if got_s is not None:
                    own[:, side] = got_s[0:16].astype(F32)
                    tb[r16(0), side] = got_s[16:32]
                go([reduce[1][i]])
            else:
                tb[pl.ds(16, 32), cols] = got.astype(BF)
                if got_s is not None:
                    tb[pl.ds(16, 32), side] = got_s
                go([reduce[3][i], reduce[2][i]])

    def total(cols):
        got = own[:, cols]
        for q in range(3):
            got = got + parts[q, :, cols].astype(F32)
        return got

    for i in range(PIECES):
        arrived([reduce[q][i] for q in (1, 2, 3)])
        cols = pl.ds(i * step, step)
        fin[:, cols] = total(cols).astype(BF)
        last[i].start()

    got = total(side)
    got = got + swap(got)
    ids_col = dot_nt(eye, ids.astype(F32).astype(BF))
    lane16 = iota((16, LANES), 1).astype(F32)
    for k in range(2):
        col = jnp.sum(
            jnp.where(lane16 == ids_col[:, k : k + 1], got, 0.0), axis=1, keepdims=True
        )
        route_v[k : k + 1, :] = jnp.sum(
            jnp.where(iota((16, 16), 0) == iota((16, 16), 1), col, 0.0),
            axis=0, keepdims=True,
        )
    route_out = pltpu.make_async_copy(route_v, route.at[0], local.at[7])
    route_out.start()
    finish()
    route_out.wait()


def hand_on(grad_in, route_in, grad_out, route_out, done):
    copies = [
        pltpu.make_async_copy(grad_in, grad_out, done.at[0]),
        pltpu.make_async_copy(route_in, route_out, done.at[1]),
    ]
    for c in copies:
        c.start()
    for c in copies:
        c.wait()


def on_device(tokens_in, out_grad, expert_ids, gate_weights, w_gate, w_up, w_down):
    D = tokens_in.shape[2]
    W = w_gate.shape[1]
    wide, back = 2 * D + LANES, D + LANES
    anywhere = pl.BlockSpec(memory_space=pl.ANY)
    hbm = pl.BlockSpec(memory_space=pltpu.HBM)
    ids = jnp.swapaxes(expert_ids, 1, 2)
    grad, route = pl.pallas_call(
        kernel,
        out_shape=(
            jax.ShapeDtypeStruct(tokens_in.shape, BF),
            jax.ShapeDtypeStruct(ids.shape, F32),
        ),
        in_specs=[hbm] * 7,
        out_specs=(anywhere, anywhere),
        scratch_shapes=[
            pltpu.VMEM((64, wide), BF),
            pltpu.VMEM((2, 48, wide), BF),
            pltpu.VMEM((128, wide), BF),
            pltpu.VMEM((4 * W, D), BF),
            pltpu.VMEM((2 * W, D), BF),
            pltpu.VMEM((4 * W, 64), F32),
            pltpu.VMEM((2, 48, back), BF),
            pltpu.VMEM((128, back), BF),
            pltpu.VMEM((48, back), BF),
            pltpu.VMEM((16, back), F32),
            pltpu.VMEM((3, 16, back), BF),
            pltpu.VMEM((16, D), BF),
            pltpu.VMEM((2, 16), jnp.int32),
            pltpu.VMEM((2, 16), BF),
            pltpu.VMEM((2, 16), F32),
            pltpu.SemaphoreType.DMA((COPIES,)),
            pltpu.SemaphoreType.DMA((COPIES,)),
            pltpu.SemaphoreType.DMA((8,)),
        ],
        compiler_params=pltpu.CompilerParams(
            collective_id=0, has_side_effects=True, vmem_limit_bytes=24 << 20
        ),
    )(
        *(
            pltpu.with_memory_space_constraint(v, pltpu.HBM)
            for v in (
                tokens_in, out_grad, ids, jnp.swapaxes(gate_weights, 1, 2),
                w_gate, w_up, w_down,
            )
        )
    )
    grad, route = pl.pallas_call(
        hand_on,
        out_shape=(
            jax.ShapeDtypeStruct(grad.shape, BF),
            jax.ShapeDtypeStruct(route.shape, F32),
        ),
        in_specs=[anywhere] * 2,
        out_specs=(hbm, hbm),
        scratch_shapes=[pltpu.SemaphoreType.DMA((2,))],
        compiler_params=pltpu.CompilerParams(vmem_limit_bytes=4 << 20),
    )(grad, route)
    return grad, jnp.swapaxes(route, 1, 2)


def solution(mesh):
    spec = P("section", "expert", None)
    return jax.shard_map(
        on_device, mesh=mesh, in_specs=(spec,) * 7, out_specs=(spec, spec), check_vma=False
    )
```

```python
import jax
import jax.numpy as jnp
from jax import lax
from jax.experimental import pallas as pl
from jax.experimental.pallas import tpu as pltpu
from jax.sharding import PartitionSpec as P

MESH = pl.DeviceIdType.MESH
BF = jnp.bfloat16
F32 = jnp.float32
NT = (((1,), (1,)), ((), ()))
EXPERTS = 8
Q = 8
LANES = 128
COPIES = 64
PIECES = 4


def iota(shape, dim):
    return lax.broadcasted_iota(jnp.int32, shape, dim)


def ones(mask):
    return mask.astype(F32).astype(BF)


def dot_nt(left, right):
    return lax.dot_general(left, right, NT, preferred_element_type=F32)


def resplit(total):
    high = total.astype(BF).astype(F32)
    lane = iota(total.shape, 1)
    return jnp.where(lane < 64, high, total - high).astype(BF)


def kernel(
    x_in, dy_in, ids_in, gw_in, wg_in, wu_in, wd_in, out, route,
    blk, sel, xin, w1, w2, acc, res, rr, tb, own, parts, fin,
    ids_v, gates_v, route_v, send, recv, local,
):
    D = x_in.shape[2]
    W = wg_in.shape[1]
    sec = lax.axis_index("section")
    secs = lax.axis_size("section")
    me = lax.axis_index("expert")
    core = me % 2
    y = (me // 2) % 4
    x = me // 8
    first = core * y + (1 - core) * x
    second = core * x + (1 - core) * y
    step_a = 8 - 6 * core
    step_b = 2 + 6 * core

    def at(pos_a, pos_b):
        return (sec, core + step_a * (pos_a % 4) + step_b * (pos_b % 4))

    a_up, a_dn, a_op = [at(first + k, second) for k in (1, 3, 2)]
    b_up, b_dn, b_op = [at(first, second + k) for k in (1, 3, 2)]
    sib = (sec, me + 1 - 2 * core)
    z_dn = ((sec + secs - 1) % secs, me)
    z_up = ((sec + 1) % secs, me)
    own_e = me // 4

    def expert_at(pos_b):
        pos_b = pos_b % 4
        return (1 - core) * (x * 2 + pos_b // 2) + core * (pos_b * 2 + y // 2)

    peers = [expert_at(second + off) for off in (0, 1, 3, 2)]

    flying, landing = {}, {}

    class Push:
        def __init__(self, src, dst, dev):
            self.i = Push.count
            Push.count += 1
            self.copy = pltpu.make_async_remote_copy(
                src_ref=src, dst_ref=dst, send_sem=send.at[self.i],
                recv_sem=recv.at[self.i], device_id=dev, device_id_type=MESH,
            )

        def start(self):
            self.copy.start()
            flying[self.i] = landing[self.i] = self.copy

        def wait(self):
            self.copy.wait_recv()
            landing.pop(self.i)

    Push.count = 0

    def go(copies):
        for c in copies:
            c.start()

    def arrived(copies):
        for c in copies:
            c.wait()

    def finish():
        for c in landing.values():
            c.wait_recv()
        for c in flying.values():
            c.wait_send()

    r16 = lambda i: pl.ds(16 * i, 16)
    side = pl.ds(D, LANES)
    head = pl.ds(0, LANES)
    parts_in = (pl.ds(0, LANES + D), pl.ds(LANES + D, D))
    step = D // PIECES
    piece = [
        pl.ds(i * step, step + (LANES if i == PIECES - 1 else 0)) for i in range(PIECES)
    ]

    barrier = pltpu.get_barrier_semaphore()
    around = (a_up, a_dn, a_op, b_up, b_dn, b_op, sib, z_dn, z_up)
    for dev in around:
        pl.semaphore_signal(barrier, inc=1, device_id=dev, device_id_type=MESH)

    loads = [
        pltpu.make_async_copy(s, d, local.at[i])
        for i, (s, d) in enumerate(
            [
                (ids_in.at[0], ids_v),
                (gw_in.at[0], gates_v),
                (x_in.at[0], blk.at[r16(0), pl.ds(LANES, D)]),
                (dy_in.at[0], blk.at[r16(0), pl.ds(LANES + D, D)]),
                (wg_in.at[0], w1.at[pl.ds(0, W)]),
                (wu_in.at[0], w1.at[pl.ds(2 * W, W)]),
                (wd_in.at[0], w2.at[pl.ds(0, W)]),
            ]
        )
    ]
    for c in loads:
        c.start()

    loads[0].wait()
    loads[1].wait()
    ids = ids_v[...]
    gates = gates_v[...].astype(F32)
    eye = ones(iota((16, 16), 0) == iota((16, 16), 1))
    row_e = iota((LANES, 16), 0)
    table = jnp.zeros((LANES, 16), F32)
    for k in range(2):
        table = table + jnp.where(row_e == ids[k : k + 1], gates[k : k + 1], 0.0)
    blk[r16(0), head] = dot_nt(eye, table.astype(BF)).astype(BF)

    pl.semaphore_wait(barrier, len(around))
    loads[2].wait()

    gather = [
        [
            Push(blk.at[r16(0), cols], blk.at[r16(q), cols], dev)
            for q, dev in ((1, a_up), (2, a_dn), (3, a_op))
        ]
        for cols in parts_in
    ]
    go(gather[0][:2])
    loads[3].wait()
    go(gather[1][:2] + [gather[0][2], gather[1][2]])
    halves = [
        Push(wg_in.at[0], w1.at[pl.ds(W, W)], sib),
        Push(wu_in.at[0], w1.at[pl.ds(3 * W, W)], sib),
        Push(wd_in.at[0], w2.at[pl.ds(W, W)], sib),
    ]
    go(halves)

    def of_peer(index):
        e = jnp.full(index.shape, peers[3], jnp.int32)
        for j in (2, 1, 0):
            e = jnp.where(index == j, peers[j], e)
        return e

    def cut(size, want):
        return max(d for d in range(LANES, want + 1, LANES) if size % d == 0)

    r32, c32 = iota((32, 32), 0), iota((32, 32), 1)
    lower = ones((r32 // 16 == c32 // 16) & (c32 < r32))
    pick = ones(iota((64, LANES), 1) == of_peer(iota((64, LANES), 0) // 16))

    def routing(g):
        hit = ones(blk[pl.ds(32 * g, 32), head].astype(F32) > 0.0)
        return hit, jnp.dot(lower, hit, preferred_element_type=F32).astype(BF)

    def selection(g):
        hit, rank = routing(g)
        r, c = iota((64, 32), 0), iota((64, 32), 1)
        good = (dot_nt(pick, hit) > 0.5) & (dot_nt(pick, rank) == (r % 8).astype(F32))
        return ones(good & ((r // 8) % 2 == c // 16))

    def select(g, perm, part):
        start, size = part.start, part.size
        width = cut(size, 1408)

        @pl.loop(0, size // width)
        def _(i):
            cols = pl.ds(pl.multiple_of(start + i * width, LANES), width)
            got = jnp.dot(
                perm, blk[pl.ds(32 * g, 32), cols], preferred_element_type=F32
            ).astype(BF)
            xin[r16(4 * g), cols] = got[0:16]
            sel[g, :, cols] = got[16:64]

    def placing(g):
        hit, rank = routing(g)
        r, c = iota((32, 64), 0), iota((32, 64), 1)
        good = (dot_nt(hit, pick) > 0.5) & (dot_nt(rank, pick) == (c % 8).astype(F32))
        return ones(good & ((c // 8) % 2 == r // 16))

    def dispatch(g):
        return [
            [
                Push(sel.at[g, r16(j - 1), cols], xin.at[r16(4 * g + j), cols], dev)
                for j, dev in ((1, b_up), (2, b_dn), (3, b_op))
            ]
            for cols in parts_in
        ]

    sent = [dispatch(0), dispatch(1)]
    back = [
        [
            [
                Push(res.at[g, r16(j - 1), cols], rr.at[r16(4 * g + j), cols], dev)
                for j, dev in ((3, b_op), (1, b_dn), (2, b_up))
            ]
            for cols in piece
        ]
        for g in range(2)
    ]
    reduce = {
        q: [Push(tb.at[r16(q - 1), cols], parts.at[q - 1, :, cols], dev) for cols in piece]
        for q, dev in ((1, a_dn), (2, a_up), (3, a_op))
    }
    last = [
        Push(fin.at[:, pl.ds(i * step, step)], out.at[0, :, pl.ds(i * step, step)], z_dn)
        for i in range(PIECES)
    ]

    for g in range(2):
        mine = (lambda k: [gather[k][0]]) if g == 0 else (lambda k: gather[k][1:])
        arrived(mine(0))
        perm = selection(g)
        select(g, perm, parts_in[0])
        go(sent[g][0])
        arrived(mine(1))
        select(g, perm, parts_in[1])
        go(sent[g][1])
    place = [placing(0), placing(1)]

    for c in loads[4:]:
        c.wait()
    arrived(halves)
    tall = 2 * W

    def experts(g):
        rows = pl.ds(64 * g, 64)
        arrived(sent[g][0])

        @pl.loop(0, 2)
        def _(k):
            units = pl.ds(pl.multiple_of(k * tall, tall), tall)
            acc[units] = dot_nt(w1[units], xin[rows, pl.ds(LANES, D)])

        arrived(sent[g][1])
        hidden = dot_nt(w2[...], xin[rows, pl.ds(LANES + D, D)])
        gate_pre = acc[0:tall]
        up_pre = acc[tall : 2 * tall]
        chosen = ones(iota((16, LANES), 1) == own_e)
        gate = dot_nt(chosen, xin[rows, head])[0:1]
        sig = jax.nn.sigmoid(gate_pre)
        act = gate_pre * sig
        slope = sig * (1.0 + gate_pre * (1.0 - sig))
        score = jnp.sum(act * up_pre * hidden, axis=0, keepdims=True)
        scaled = hidden * gate
        grads = jnp.concatenate(
            [
                jnp.transpose(scaled * up_pre * slope).astype(BF),
                jnp.transpose(scaled * act).astype(BF),
            ],
            axis=1,
        )
        score = jnp.sum(
            jnp.where(iota((64, 64), 0) == iota((64, 64), 1), score, 0.0),
            axis=1, keepdims=True,
        )
        lane = iota((64, LANES), 1)
        scores = resplit(jnp.where((lane % 64) == own_e, score, 0.0))
        rr[r16(4 * g), side] = scores[0:16]
        res[g, :, side] = scores[16:64]
        width = cut(step, 512)
        for i in range(PIECES):

            @pl.loop(0, step // width)
            def _(k):
                cols = pl.ds(pl.multiple_of(i * step + k * width, LANES), width)
                got = jnp.dot(
                    grads, w1[:, cols], preferred_element_type=F32
                ).astype(BF)
                rr[r16(4 * g), cols] = got[0:16]
                res[g, :, cols] = got[16:64]

            go(back[g][i])

    experts(0)
    experts(1)

    swap = lambda v: pltpu.roll(v, 64, 1)
    for g in range(2):
        rows = pl.ds(64 * g, 64)
        for i in range(PIECES):
            arrived(back[g][i])
            cols = pl.ds(i * step, step)
            got = jnp.dot(place[g], rr[rows, cols], preferred_element_type=F32)
            got_s = None
            if i == PIECES - 1:
                got_s = jnp.dot(place[g], rr[rows, side], preferred_element_type=F32)
                got_s = resplit(got_s + swap(got_s))
            if g == 0:
                own[:, cols] = got[0:16]
                tb[r16(0), cols] = got[16:32].astype(BF)
                if got_s is not None:
                    own[:, side] = got_s[0:16].astype(F32)
                    tb[r16(0), side] = got_s[16:32]
                go([reduce[1][i]])
            else:
                tb[pl.ds(16, 32), cols] = got.astype(BF)
                if got_s is not None:
                    tb[pl.ds(16, 32), side] = got_s
                go([reduce[3][i], reduce[2][i]])

    def total(cols):
        got = own[:, cols]
        for q in range(3):
            got = got + parts[q, :, cols].astype(F32)
        return got

    for i in range(PIECES):
        arrived([reduce[q][i] for q in (1, 2, 3)])
        cols = pl.ds(i * step, step)
        fin[:, cols] = total(cols).astype(BF)
        last[i].start()

    got = total(side)
    got = got + swap(got)
    ids_col = dot_nt(eye, ids.astype(F32).astype(BF))
    lane16 = iota((16, LANES), 1).astype(F32)
    for k in range(2):
        col = jnp.sum(
            jnp.where(lane16 == ids_col[:, k : k + 1], got, 0.0), axis=1, keepdims=True
        )
        route_v[k : k + 1, :] = jnp.sum(
            jnp.where(iota((16, 16), 0) == iota((16, 16), 1), col, 0.0),
            axis=0, keepdims=True,
        )
    route_out = pltpu.make_async_copy(route_v, route.at[0], local.at[7])
    route_out.start()
    finish()
    route_out.wait()


def hand_on(grad_in, route_in, grad_out, route_out, done):
    copies = [
        pltpu.make_async_copy(grad_in, grad_out, done.at[0]),
        pltpu.make_async_copy(route_in, route_out, done.at[1]),
    ]
    for c in copies:
        c.start()
    for c in copies:
        c.wait()


def on_device(tokens_in, out_grad, expert_ids, gate_weights, w_gate, w_up, w_down):
    D = tokens_in.shape[2]
    W = w_gate.shape[1]
    wide, back = 2 * D + LANES, D + LANES
    anywhere = pl.BlockSpec(memory_space=pl.ANY)
    hbm = pl.BlockSpec(memory_space=pltpu.HBM)
    ids = jnp.swapaxes(expert_ids, 1, 2)
    grad, route = pl.pallas_call(
        kernel,
        out_shape=(
            jax.ShapeDtypeStruct(tokens_in.shape, BF),
            jax.ShapeDtypeStruct(ids.shape, F32),
        ),
        in_specs=[hbm] * 7,
        out_specs=(anywhere, anywhere),
        scratch_shapes=[
            pltpu.VMEM((64, wide), BF),
            pltpu.VMEM((2, 48, wide), BF),
            pltpu.VMEM((128, wide), BF),
            pltpu.VMEM((4 * W, D), BF),
            pltpu.VMEM((2 * W, D), BF),
            pltpu.VMEM((4 * W, 64), F32),
            pltpu.VMEM((2, 48, back), BF),
            pltpu.VMEM((128, back), BF),
            pltpu.VMEM((48, back), BF),
            pltpu.VMEM((16, back), F32),
            pltpu.VMEM((3, 16, back), BF),
            pltpu.VMEM((16, D), BF),
            pltpu.VMEM((2, 16), jnp.int32),
            pltpu.VMEM((2, 16), BF),
            pltpu.VMEM((2, 16), F32),
            pltpu.SemaphoreType.DMA((COPIES,)),
            pltpu.SemaphoreType.DMA((COPIES,)),
            pltpu.SemaphoreType.DMA((8,)),
        ],
        compiler_params=pltpu.CompilerParams(
            collective_id=0, has_side_effects=True, vmem_limit_bytes=24 << 20
        ),
    )(
        *(
            pltpu.with_memory_space_constraint(v, pltpu.HBM)
            for v in (
                tokens_in, out_grad, ids, jnp.swapaxes(gate_weights, 1, 2),
                w_gate, w_up, w_down,
            )
        )
    )
    grad, route = pl.pallas_call(
        hand_on,
        out_shape=(
            jax.ShapeDtypeStruct(grad.shape, BF),
            jax.ShapeDtypeStruct(route.shape, F32),
        ),
        in_specs=[anywhere] * 2,
        out_specs=(hbm, hbm),
        scratch_shapes=[pltpu.SemaphoreType.DMA((2,))],
        compiler_params=pltpu.CompilerParams(vmem_limit_bytes=4 << 20),
    )(grad, route)
    return grad, jnp.swapaxes(route, 1, 2)


def solution(mesh):
    spec = P("section", "expert", None)
    return jax.shard_map(
        on_device, mesh=mesh, in_specs=(spec,) * 7, out_specs=(spec, spec), check_vma=False
    )
```
